256 devices in a mesh: band: 32 (over y, z), chan: 8 (over x, core).
Axes of the slice: x: 4, y: 4, z: 8, core: 2. Of those that a mesh axis runs over, the one named last changes fastest.
Arguments:
- new_frames: bfloat16 [4, 128, 512, 320], P(None, 'band', 'chan'), may hold values from -6 to 6
- cached_frames: bfloat16 [2, 128, 512, 320], P(None, 'band', 'chan'), may hold values from -6 to 6
- conv_weight: bfloat16 [3, 3, 3, 512, 512], P(None, None, None, 'chan'), may hold values from -0.0546875 to 0.0546875
- out_bias: float32 [512], P('chan'), may hold values from -3 to 3
Outputs:
- conv_out: bfloat16 [4, 128, 512, 320], P(None, 'band', 'chan')
The draws below stay inside these ranges and needn't reach their ends.
All inputs are finite; a program needn't handle non-finite values.
Results may differ from the reference program's by a relative error of at most 0.001.
Values may be sent and summed in bfloat16 or wider, within the bound.
No kernel may reach another device: no remote copies, remote signals or barrier semaphores. Data moves between devices by JAX's collectives and lax.ppermute only.
A program may use at most 128 MiB of HBM per device.

```python
import jax
import jax.numpy as jnp

C = 512
W = 320
FRAMES = 4
CACHE = 2
H = 128


def shard_levels(rng, extent, shards, least, top_value):
    level, own = 1.0, jax.random.fold_in(rng, 6)
    for axis_at, shards_of in shards:
        steps = jnp.exp(jax.random.uniform(jax.random.fold_in(own, axis_at), (shards_of,), jnp.float32, least / len(shards), top_value / len(shards)))
        level = level * jnp.repeat(steps, extent[axis_at] // shards_of).reshape([-1 if axis == axis_at else 1 for axis in range(len(extent))])
    return level


def scatter_about(own_key, shape, deviation, reach, shards=(), dtype=jnp.bfloat16):
    values = jax.random.normal(own_key, shape, jnp.float32) * deviation
    if len(shards) > 0:
        values = shard_levels(own_key, shape, shards, -0.22, 0.18) * values
    return jnp.clip(values, min=-reach, max=reach).astype(dtype)


def setup_inputs(seed: int = 0) -> dict:
    key_list = jax.random.split(jax.random.key(seed), 5)
    return {
        "new_frames": scatter_about(key_list[0], (FRAMES, H, C, W), 1.0, 6.0, ((1, 32), (2, 8))),
        "cached_frames": scatter_about(key_list[1], (CACHE, H, C, W), 1.0, 6.0, ((1, 32), (2, 8))),
        "conv_weight": scatter_about(key_list[2], (3, 3, 3, C, C), (27 * C) ** -0.5, 0.0546875, ((3, 8),)),
        "out_bias": scatter_about(key_list[3], (C,), 0.5, 3.0, ((0, 8),), jnp.float32),
    }


def reference(new_frames, cached_frames, conv_weight, out_bias):
    stacked = jnp.concatenate([cached_frames, new_frames], axis=0).astype(jnp.float32)
    padded = jnp.pad(stacked, ((0, 0), (1, 1), (0, 0), (1, 1)))
    weights_wide = conv_weight.astype(jnp.float32)
    frame_count = new_frames.shape[0]
    row_count = new_frames.shape[1]
    col_count = new_frames.shape[3]
    summed = jnp.zeros((frame_count, row_count, conv_weight.shape[3], col_count), jnp.float32)
    for time_tap in range(3):
        for row_tap in range(3):
            for col_tap in range(3):
                window = padded[time_tap:time_tap + frame_count, row_tap:row_tap + row_count, :, col_tap:col_tap + col_count]
                summed = summed + jnp.einsum("dc,frcw->frdw", weights_wide[time_tap, row_tap, col_tap], window)
    return (summed + out_bias.astype(jnp.float32)[None, None, :, None]).astype(jnp.bfloat16)
```

```python
import functools

import jax
import jax.numpy as jnp
from jax import lax
from jax.experimental import pallas as pl
from jax.experimental.pallas import tpu as pltpu
from jax.sharding import PartitionSpec as P


BF = jnp.bfloat16
F32 = jnp.float32
LANES = 128


def roll_half(packed):
    half = packed.shape[-1] // 2
    return pltpu.roll(packed.astype(F32), half, axis=packed.ndim - 1).astype(BF)


def block_kernel(plan, cols, first, last, *refs):
    scalars, refs = refs[0], list(refs[1:])
    slots = 1 + max(slot for slot, _, _ in plan)
    pieces = [(refs.pop(0), refs.pop(0), refs.pop(0)) for _ in plan]
    weights = [(refs.pop(0), refs.pop(0)) for _ in range(slots)]
    before = None if first else refs.pop(0)
    bias = refs.pop(0) if last else None
    outs = [refs.pop(0), refs.pop(0)] if last else [refs.pop(0)]
    xs, ws = refs
    depth = slots * LANES
    frame = pl.program_id(0)
    core = scalars[0]
    width = 2 * cols

    @pl.when(frame == 0)
    def _():
        near = lax.broadcasted_iota(jnp.int32, (LANES, width), 1) < cols
        for (slot, start, count), (pair, zside, cside) in zip(plan, pieces):

            def one(g, carry, slot=slot, start=start, pair=pair, zside=zside, cside=cside):
                here = pair[g]
                turned = roll_half(here)
                zrow = jnp.concatenate([zside[g], jnp.zeros((LANES, width - zside.shape[-1]), BF)], axis=1)
                crow = jnp.concatenate([jnp.zeros((LANES, width - cside.shape[-1]), BF), cside[g]], axis=1)
                base = (start + g) * 3 * depth + slot * LANES
                base = pl.multiple_of(base, LANES)
                xs[pl.ds(base, LANES), :] = jnp.where(near, zrow, turned)
                xs[pl.ds(pl.multiple_of(base + depth, LANES), LANES), :] = here
                xs[pl.ds(pl.multiple_of(base + 2 * depth, LANES), LANES), :] = jnp.where(near, turned, crow)
                return carry

            lax.fori_loop(0, count, one, 0)
        for t in range(3):
            for delta in range(3):
                row_tap = jnp.where(core == 0, delta, 2 - delta)
                for slot in range(slots):
                    at = ((t * 3 + delta) * slots + slot) * LANES
                    for half in range(2):
                        w = weights[slot][half][t, row_tap]
                        rows = w.shape[0] * w.shape[1]
                        ws[half * rows : (half + 1) * rows, at : at + LANES] = w.reshape(rows, LANES)

    window = xs[pl.ds(pl.multiple_of(frame * 3 * depth, LANES), 9 * depth), :]
    acc = jnp.dot(ws[...], window, preferred_element_type=F32)
    if not first:
        acc = acc + before[0]
    if not last:
        outs[0][0] = acc
        return
    lane = lax.broadcasted_iota(jnp.int32, (acc.shape[0] // 6, width), 1)
    zero = jnp.zeros((acc.shape[0] // 6, width), F32)
    left_edge = (lane == 0) | (lane == cols)
    right_edge = (lane == cols - 1) | (lane == width - 1)
    rows = acc.shape[0] // 6
    for half in range(2):
        part = acc[half * 3 * rows : (half + 1) * 3 * rows]
        from_left = jnp.where(left_edge, zero, pltpu.roll(part[:rows], 1, axis=1))
        from_right = jnp.where(right_edge, zero, pltpu.roll(part[2 * rows :], width - 1, axis=1))
        total = part[rows : 2 * rows] + from_left + from_right + bias[half][:, None]
        outs[half][0] = total.astype(BF)


def block_call(plan, cols, scalars, pieces, weights, before, bias, name):
    first, last = before is None, bias is not None
    slots = 1 + max(slot for slot, _, _ in plan)
    own, other = weights
    taps, outs64 = own.shape[:3], own.shape[3]
    rows = 2 * 3 * outs64
    width = 2 * cols
    depth = slots * LANES
    frames = 4
    operands, specs = [], []
    for piece in pieces:
        for array in piece:
            operands.append(array)
            specs.append(pl.BlockSpec(array.shape, lambda f, s, n=array.ndim: (0,) * n))
    for slot in range(slots):
        for array in (own, other):
            operands.append(array)
            specs.append(pl.BlockSpec((*taps, outs64, LANES), lambda f, s, slot=slot: (0, 0, 0, 0, s[1 + slot])))
    if not first:
        operands.append(before)
        specs.append(pl.BlockSpec((1, rows, width), lambda f, s: (f, 0, 0)))
    if last:
        operands.append(bias)
        specs.append(pl.BlockSpec(bias.shape, lambda f, s: (0, 0)))
        out_shape = [jax.ShapeDtypeStruct((frames, outs64, width), BF)] * 2
        out_specs = [pl.BlockSpec((1, outs64, width), lambda f, s: (f, 0, 0))] * 2
    else:
        out_shape = jax.ShapeDtypeStruct((frames, rows, width), F32)
        out_specs = pl.BlockSpec((1, rows, width), lambda f, s: (f, 0, 0))
    flops = 2 * frames * rows * 9 * depth * width
    return pl.pallas_call(
        functools.partial(block_kernel, plan, cols, first, last),
        grid_spec=pltpu.PrefetchScalarGridSpec(
            num_scalar_prefetch=1,
            grid=(frames,),
            in_specs=specs,
            out_specs=out_specs,
            scratch_shapes=[
                pltpu.VMEM((6 * 3 * depth, width), BF),
                pltpu.VMEM((rows, 9 * depth), BF),
            ],
        ),
        out_shape=out_shape,
        compiler_params=pltpu.CompilerParams(vmem_limit_bytes=40 * 2**20),
        cost_estimate=pl.CostEstimate(flops=flops, bytes_accessed=8 * 2**20, transcendentals=0),
        name=name,
    )(scalars, *operands)


def solution(mesh):
    bands, chans = mesh.shape["band"], mesh.shape["chan"]
    chips = chans // 2
    swap = [(2 * x + c, 2 * x + 1 - c) for x in range(chips) for c in range(2)]
    right = [(2 * x + c, 2 * ((x + 1) % chips) + c) for x in range(chips) for c in range(2)]
    left = [(target, source) for source, target in right]
    across = []
    for b in range(1, bands):
        for x in range(chips):
            low, high = b * chans + 2 * x, (b - 1) * chans + 2 * x + 1
            across += [(low, high), (high, low)]

    def on_device(new_frames, cached_frames, conv_weight, out_bias):
        cols = new_frames.shape[-1]
        index = lax.axis_index("chan")
        core, chip = index % 2, index // 2
        even = core == 0

        def swapped(a):
            return lax.ppermute(a, "chan", swap)

        def pack(a, keep):
            pick = even if keep else jnp.logical_not(even)
            outer = jnp.where(pick, a[:, 0], a[:, 3])
            inner = jnp.where(pick, a[:, 1], a[:, 2])
            return jnp.concatenate([outer, inner], axis=-1)

        def halos(pair):
            zside = lax.ppermute(pair[:, :, : 3 * LANES], ("band", "chan"), across)
            cside = swapped(pair[:, :, -3 * LANES :])
            return pair, zside, cside

        stacked = jnp.concatenate([cached_frames, new_frames], axis=0)
        sent = swapped(pack(stacked, False))
        kept = pack(stacked, True)
        own = jnp.where(even, jnp.concatenate([kept, sent], axis=1), jnp.concatenate([sent, kept], axis=1))
        other_weight = swapped(conv_weight)
        biases = jnp.stack([out_bias, swapped(out_bias)])
        lo, hi = own[:3], own[3:]
        l_lo = lax.ppermute(lo, "chan", right)
        r_hi = lax.ppermute(hi, "chan", left)
        l_hi = lax.ppermute(hi, "chan", right)
        r_lo = lax.ppermute(lo, "chan", left)
        f_lo = lax.ppermute(l_lo, "chan", right)
        f_hi = lax.ppermute(r_hi, "chan", left)

        weights = (conv_weight, other_weight)

        def scalars(*offsets):
            return jnp.stack([core] + [(chip + o) % chips for o in offsets]).astype(jnp.int32)

        acc = block_call([(0, 0, 6)], cols, scalars(0), [halos(own)], weights, None, None, "own")
        acc = block_call(
            [(0, 0, 3), (1, 3, 3), (0, 3, 3), (1, 0, 3)], cols, scalars(chips - 1, 1),
            [halos(l_lo), halos(r_hi), halos(l_hi), halos(r_lo)], weights, acc, None, "sides",
        )
        mine, theirs = block_call(
            [(0, 0, 3), (0, 3, 3)], cols, scalars(2), [halos(f_lo), halos(f_hi)], weights, acc, biases, "far"
        )
        got = swapped(theirs)
        m0, m1, g0, g1 = mine[..., :cols], mine[..., cols:], got[..., :cols], got[..., cols:]
        return jnp.stack(
            [jnp.where(even, m0, g0), jnp.where(even, m1, g1), jnp.where(even, g1, m1), jnp.where(even, g0, m0)], axis=1
        )

    in_specs = (
        P(None, "band", "chan", None),
        P(None, "band", "chan", None),
        P(None, None, None, "chan", None),
        P("chan"),
    )
    return jax.shard_map(
        on_device, mesh=mesh, in_specs=in_specs, out_specs=P(None, "band", "chan", None), check_vma=False
    )
```

```python
import functools

import jax
import jax.numpy as jnp
from jax import lax
from jax.experimental import pallas as pl
from jax.experimental.pallas import tpu as pltpu
from jax.sharding import PartitionSpec as P


BF = jnp.bfloat16
F32 = jnp.float32
LANES = 128
HALF = 64


def turn(pairs):
    width = pairs.shape[-1]
    return pltpu.roll(pairs.astype(F32), width // 2, axis=1)


def pack_kernel(flip_ref, cached_ref, new_ref, kept_ref, sent_ref):
    cols = cached_ref.shape[-1]
    upper = flip_ref[0]
    place = [
        (lax.broadcasted_iota(jnp.int32, (cols, 2 * cols), 0) + h * cols
         == lax.broadcasted_iota(jnp.int32, (cols, 2 * cols), 1)).astype(F32).astype(BF)
        for h in range(2)
    ]
    for out, flip in ((kept_ref, upper), (sent_ref, 1 - upper)):
        for row in range(2):
            at = jnp.where(flip == 0, row, 3 - row)
            for pair in range(3):
                first = cached_ref[0, at] if pair == 0 else new_ref[2 * pair - 2, at]
                second = cached_ref[1, at] if pair == 0 else new_ref[2 * pair - 1, at]
                both = jnp.dot(first, place[0], preferred_element_type=F32)
                both = both + jnp.dot(second, place[1], preferred_element_type=F32)
                out[row, pair] = both.astype(BF)


def pack(flip, cached, new):
    channels, cols = cached.shape[2:]
    shape = jax.ShapeDtypeStruct((2, 3, channels, 2 * cols), BF)
    return pl.pallas_call(
        pack_kernel,
        in_specs=[pl.BlockSpec(memory_space=pltpu.SMEM)] + [pl.BlockSpec(memory_space=pltpu.VMEM)] * 2,
        out_specs=[pl.BlockSpec(memory_space=pltpu.VMEM)] * 2,
        out_shape=[shape, shape],
        compiler_params=pltpu.CompilerParams(vmem_limit_bytes=16 * 2**20),
        cost_estimate=pl.CostEstimate(flops=10**8, bytes_accessed=4 * 2**20, transcendentals=0),
        name="pack",
    )(flip, cached, new)


def block_kernel(mixed, first, last, *refs):
    scalars, refs = refs[0], list(refs[1:])
    bodies = [refs.pop(0), refs.pop(0)]
    zsides = [refs.pop(0), refs.pop(0)]
    csides = [refs.pop(0), refs.pop(0)]
    weights = [(refs.pop(0), refs.pop(0)) for _ in range(2 if mixed else 1)]
    before = None if first else refs.pop(0)
    bias = refs.pop(0) if last else None
    outs = [refs.pop(0), refs.pop(0)] if last else [refs.pop(0)]
    (xs,) = refs
    p = pl.program_id(0)
    flip = scalars[0]
    width = xs.shape[-1]
    cols = width // 2
    near = lax.broadcasted_iota(jnp.int32, (HALF, width), 1) < cols
    for piece in range(2):
        at = pl.ds(piece * HALF, HALF)
        rows = [
            lambda q: zsides[piece][q],
            lambda q: bodies[piece][0, q],
            lambda q: bodies[piece][1, q],
            lambda q: csides[piece][q],
        ]
        for row in range(4):
            low, high = rows[row](p), rows[row](p + 1)
            xs[0, row, at] = low
            xs[2, row, at] = high
            xs[1, row, at] = jnp.where(near, turn(low), turn(high)).astype(BF)

    channel = lax.broadcasted_iota(jnp.int32, (1, LANES), 1)
    from_first = channel < HALF
    taps = []
    for t in range(3):
        for delta in range(3):
            row_tap = jnp.where(flip == 0, delta, 2 - delta)
            halves = []
            for half in range(2):
                w = weights[0][half][t, row_tap]
                w = w.reshape(w.shape[0] * w.shape[1], LANES)
                if mixed:
                    v = weights[1][half][t, row_tap].reshape(w.shape)
                    w = jnp.where(jnp.broadcast_to(from_first, w.shape), w, v)
                halves.append(w)
            taps.append(jnp.concatenate(halves, axis=0))
    lhs = jnp.concatenate(taps, axis=1)
    rows = lhs.shape[0] // 6
    lane = lax.broadcasted_iota(jnp.int32, (rows, width), 1)
    zero = jnp.zeros((rows, width), F32)
    left_edge = (lane == 0) | (lane == cols)
    right_edge = (lane == cols - 1) | (lane == width - 1)
    for row in range(2):
        window = jnp.concatenate(
            [xs[t, row : row + 3].reshape(3 * LANES, width) for t in range(3)], axis=0
        )
        acc = jnp.dot(lhs, window, preferred_element_type=F32)
        if not first:
            acc = acc + before[0, row]
        if not last:
            outs[0][0, row] = acc
            continue
        for half in range(2):
            part = acc[half * 3 * rows : (half + 1) * 3 * rows]
            from_left = jnp.where(left_edge, zero, pltpu.roll(part[:rows], 1, axis=1))
            from_right = jnp.where(right_edge, zero, pltpu.roll(part[2 * rows :], width - 1, axis=1))
            total = part[rows : 2 * rows] + from_left + from_right + bias[half][:, None]
            outs[half][0, row] = total.astype(BF)


def block_call(scalars, bodies, zsides, csides, weights, mixed, before, bias, name):
    first, last = before is None, bias is not None
    own, other = weights
    taps, outs64 = own.shape[:3], own.shape[3]
    rows = 2 * 3 * outs64
    width = bodies[0].shape[-1]
    operands = [*bodies, *zsides, *csides]
    specs = [pl.BlockSpec(a.shape, lambda p, s, n=a.ndim: (0,) * n) for a in operands]
    for slot in range(2 if mixed else 1):
        for array in (own, other):
            operands.append(array)
            specs.append(pl.BlockSpec((*taps, outs64, LANES), lambda p, s, slot=slot: (0, 0, 0, 0, s[1 + slot])))
    if not first:
        operands.append(before)
        specs.append(pl.BlockSpec((1, 2, rows, width), lambda p, s: (p, 0, 0, 0)))
    if last:
        operands.append(bias)
        specs.append(pl.BlockSpec(bias.shape, lambda p, s: (0, 0)))
        out_shape = [jax.ShapeDtypeStruct((2, 2, outs64, width), BF)] * 2
        out_specs = [pl.BlockSpec((1, 2, outs64, width), lambda p, s: (p, 0, 0, 0))] * 2
    else:
        out_shape = jax.ShapeDtypeStruct((2, 2, rows, width), F32)
        out_specs = pl.BlockSpec((1, 2, rows, width), lambda p, s: (p, 0, 0, 0))
    return pl.pallas_call(
        functools.partial(block_kernel, mixed, first, last),
        grid_spec=pltpu.PrefetchScalarGridSpec(
            num_scalar_prefetch=1,
            grid=(2,),
            in_specs=specs,
            out_specs=out_specs,
            scratch_shapes=[pltpu.VMEM((3, 4, LANES, width), BF)],
        ),
        out_shape=out_shape,
        compiler_params=pltpu.CompilerParams(vmem_limit_bytes=32 * 2**20),
        cost_estimate=pl.CostEstimate(
            flops=2 * 4 * rows * 9 * LANES * width, bytes_accessed=8 * 2**20, transcendentals=0
        ),
        name=name,
    )(scalars, *operands)


def solution(mesh):
    bands, chans = mesh.shape["band"], mesh.shape["chan"]
    chips = chans // 2
    swap = [(2 * x + c, 2 * x + 1 - c) for x in range(chips) for c in range(2)]
    right = [(2 * x + c, 2 * ((x + 1) % chips) + c) for x in range(chips) for c in range(2)]
    left = [(target, source) for source, target in right]
    across = []
    for b in range(1, bands):
        for x in range(chips):
            here, there = b * chans + 2 * x + b % 2, (b - 1) * chans + 2 * x + b % 2
            across += [(here, there), (there, here)]

    def on_device(new_frames, cached_frames, conv_weight, out_bias):
        cols = new_frames.shape[-1]
        index = lax.axis_index("chan")
        core, chip = index % 2, index // 2
        even = core == 0
        flip = (core + lax.axis_index("band")) % 2
        upper = flip == 0

        def swapped(a):
            return lax.ppermute(a, "chan", swap)

        def halos(a, b):
            z = lax.ppermute(jnp.stack([a[0], b[0]]), ("band", "chan"), across)
            c = swapped(jnp.stack([a[1], b[1]]))
            return (z[0], z[1]), (c[0], c[1])

        kept, sent = pack(flip.astype(jnp.int32).reshape(1), cached_frames, new_frames)
        got = swapped(sent)
        other_weight = swapped(conv_weight)
        biases = jnp.stack([out_bias, swapped(out_bias)])
        lo, hi = jnp.where(even, kept, got), jnp.where(even, got, kept)
        l_lo = lax.ppermute(lo, "chan", right)
        r_hi = lax.ppermute(hi, "chan", left)
        l_hi = lax.ppermute(hi, "chan", right)
        r_lo = lax.ppermute(lo, "chan", left)
        weights = (conv_weight, other_weight)

        def scalars(*offsets):
            return jnp.stack([flip] + [(chip + o) % chips for o in offsets]).astype(jnp.int32)

        acc = block_call(scalars(0), (lo, hi), *halos(lo, hi), weights, False, None, None, "own")
        l_lo, r_hi, acc = lax.optimization_barrier((l_lo, r_hi, acc))
        f_lo = lax.ppermute(l_lo, "chan", right)
        f_hi = lax.ppermute(r_hi, "chan", left)
        acc = block_call(
            scalars(chips - 1, 1), (l_lo, r_hi), *halos(l_lo, r_hi), weights, True, acc, None, "near"
        )
        f_lo, f_hi, acc = lax.optimization_barrier((f_lo, f_hi, acc))
        acc = block_call(
            scalars(1, chips - 1), (r_lo, l_hi), *halos(r_lo, l_hi), weights, True, acc, None, "late"
        )
        mine, theirs = block_call(
            scalars(2), (f_lo, f_hi), *halos(f_lo, f_hi), weights, False, acc, biases, "far"
        )
        given = swapped(theirs)

        def row(a, r):
            a = a[:, r]
            return jnp.stack([a[..., :cols], a[..., cols:]], axis=1).reshape(4, a.shape[1], cols)

        m, g = [row(mine, 0), row(mine, 1)], [row(given, 0), row(given, 1)]
        return jnp.stack([jnp.where(upper, a, b) for a, b in zip(m + g[::-1], g + m[::-1])], axis=1)

    in_specs = (
        P(None, "band", "chan", None),
        P(None, "band", "chan", None),
        P(None, None, None, "chan", None),
        P("chan"),
    )
    return jax.shard_map(
        on_device, mesh=mesh, in_specs=in_specs, out_specs=P(None, "band", "chan", None), check_vma=False
    )
```

```python
import functools

import jax
import jax.numpy as jnp
from jax import lax
from jax.experimental import pallas as pl
from jax.experimental.pallas import tpu as pltpu
from jax.sharding import PartitionSpec as P


BF = jnp.bfloat16
F32 = jnp.float32
LANES = 128
HALF = 64


def turn(pairs):
    width = pairs.shape[-1]
    return pltpu.roll(pairs.astype(F32), width // 2, axis=1)


def pack_kernel(flip_ref, cached_ref, new_ref, kept_ref, sent_ref):
    cols = cached_ref.shape[-1]
    upper = flip_ref[0]
    place = [
        (lax.broadcasted_iota(jnp.int32, (cols, 2 * cols), 0) + h * cols
         == lax.broadcasted_iota(jnp.int32, (cols, 2 * cols), 1)).astype(F32).astype(BF)
        for h in range(2)
    ]
    for out, flip in ((kept_ref, upper), (sent_ref, 1 - upper)):
        for row in range(2):
            at = jnp.where(flip == 0, row, 3 - row)
            for pair in range(3):
                first = cached_ref[0, at] if pair == 0 else new_ref[2 * pair - 2, at]
                second = cached_ref[1, at] if pair == 0 else new_ref[2 * pair - 1, at]
                both = jnp.dot(first, place[0], preferred_element_type=F32)
                both = both + jnp.dot(second, place[1], preferred_element_type=F32)
                out[row, pair] = both.astype(BF)


def pack(flip, cached, new):
    channels, cols = cached.shape[2:]
    shape = jax.ShapeDtypeStruct((2, 3, channels, 2 * cols), BF)
    return pl.pallas_call(
        pack_kernel,
        in_specs=[pl.BlockSpec(memory_space=pltpu.SMEM)] + [pl.BlockSpec(memory_space=pltpu.VMEM)] * 2,
        out_specs=[pl.BlockSpec(memory_space=pltpu.VMEM)] * 2,
        out_shape=[shape, shape],
        compiler_params=pltpu.CompilerParams(vmem_limit_bytes=16 * 2**20),
        cost_estimate=pl.CostEstimate(flops=10**8, bytes_accessed=4 * 2**20, transcendentals=0),
        name="pack",
    )(flip, cached, new)


def block_kernel(mixed, first, last, *refs):
    scalars, refs = refs[0], list(refs[1:])
    bodies = [refs.pop(0), refs.pop(0)]
    zsides = [refs.pop(0), refs.pop(0)]
    csides = [refs.pop(0), refs.pop(0)]
    weights = [(refs.pop(0), refs.pop(0)) for _ in range(2 if mixed else 1)]
    before = None if first else refs.pop(0)
    bias = refs.pop(0) if last else None
    outs = [refs.pop(0), refs.pop(0)] if last else [refs.pop(0)]
    (xs,) = refs
    p = pl.program_id(0)
    flip, edge = scalars[0], scalars[3] == 1
    width = xs.shape[-1]
    cols = width // 2
    near = lax.broadcasted_iota(jnp.int32, (HALF, width), 1) < cols
    for piece in range(2):
        at = pl.ds(piece * HALF, HALF)
        rows = [
            lambda q: jnp.where(edge, jnp.zeros((HALF, width), BF), zsides[piece][q]),
            lambda q: bodies[piece][0, q],
            lambda q: bodies[piece][1, q],
            lambda q: csides[piece][q],
        ]
        for row in range(4):
            low, high = rows[row](p), rows[row](p + 1)
            xs[0, row, at] = low
            xs[2, row, at] = high
            xs[1, row, at] = jnp.where(near, turn(low), turn(high)).astype(BF)

    channel = lax.broadcasted_iota(jnp.int32, (1, LANES), 1)
    from_first = channel < HALF
    taps = []
    for t in range(3):
        for delta in range(3):
            row_tap = jnp.where(flip == 0, delta, 2 - delta)
            halves = []
            for half in range(2):
                w = weights[0][half][t, row_tap]
                w = w.reshape(w.shape[0] * w.shape[1], LANES)
                if mixed:
                    v = weights[1][half][t, row_tap].reshape(w.shape)
                    w = jnp.where(jnp.broadcast_to(from_first, w.shape), w, v)
                halves.append(w)
            taps.append(jnp.concatenate(halves, axis=0))
    lhs = jnp.concatenate(taps, axis=1)
    rows = lhs.shape[0] // 6
    lane = lax.broadcasted_iota(jnp.int32, (rows, width), 1)
    zero = jnp.zeros((rows, width), F32)
    left_edge = (lane == 0) | (lane == cols)
    right_edge = (lane == cols - 1) | (lane == width - 1)
    for row in range(2):
        window = jnp.concatenate(
            [xs[t, row : row + 3].reshape(3 * LANES, width) for t in range(3)], axis=0
        )
        acc = jnp.dot(lhs, window, preferred_element_type=F32)
        if not first:
            acc = acc + before[0, row]
        if not last:
            outs[0][0, row] = acc
            continue
        for half in range(2):
            part = acc[half * 3 * rows : (half + 1) * 3 * rows]
            from_left = jnp.where(left_edge, zero, pltpu.roll(part[:rows], 1, axis=1))
            from_right = jnp.where(right_edge, zero, pltpu.roll(part[2 * rows :], width - 1, axis=1))
            total = part[rows : 2 * rows] + from_left + from_right + bias[half][:, None]
            outs[half][0, row] = total.astype(BF)


def block_call(scalars, bodies, zsides, csides, weights, mixed, before, bias):
    first, last = before is None, bias is not None
    own, other = weights
    taps, outs64 = own.shape[:3], own.shape[3]
    rows = 2 * 3 * outs64
    width = bodies[0].shape[-1]
    operands = [*bodies, *zsides, *csides]
    specs = [pl.BlockSpec(a.shape, lambda p, s, n=a.ndim: (0,) * n) for a in operands]
    for slot in range(2 if mixed else 1):
        for array in (own, other):
            operands.append(array)
            specs.append(pl.BlockSpec((*taps, outs64, LANES), lambda p, s, slot=slot: (0, 0, 0, 0, s[1 + slot])))
    if not first:
        operands.append(before)
        specs.append(pl.BlockSpec((1, 2, rows, width), lambda p, s: (p, 0, 0, 0)))
    if last:
        operands.append(bias)
        specs.append(pl.BlockSpec(bias.shape, lambda p, s: (0, 0)))
        out_shape = [jax.ShapeDtypeStruct((2, 2, outs64, width), BF)] * 2
        out_specs = [pl.BlockSpec((1, 2, outs64, width), lambda p, s: (p, 0, 0, 0))] * 2
    else:
        out_shape = jax.ShapeDtypeStruct((2, 2, rows, width), F32)
        out_specs = pl.BlockSpec((1, 2, rows, width), lambda p, s: (p, 0, 0, 0))
    return pl.pallas_call(
        functools.partial(block_kernel, mixed, first, last),
        grid_spec=pltpu.PrefetchScalarGridSpec(
            num_scalar_prefetch=1,
            grid=(2,),
            in_specs=specs,
            out_specs=out_specs,
            scratch_shapes=[pltpu.VMEM((3, 4, LANES, width), BF)],
        ),
        out_shape=out_shape,
        compiler_params=pltpu.CompilerParams(vmem_limit_bytes=32 * 2**20),
        cost_estimate=pl.CostEstimate(
            flops=2 * 4 * rows * 9 * LANES * width, bytes_accessed=8 * 2**20, transcendentals=0
        ),
    )(scalars, *operands)


def solution(mesh):
    bands, chans = mesh.shape["band"], mesh.shape["chan"]
    chips = chans // 2
    swap = [(2 * x + c, 2 * x + 1 - c) for x in range(chips) for c in range(2)]
    right = [(2 * x + c, 2 * ((x + 1) % chips) + c) for x in range(chips) for c in range(2)]
    left = [(target, source) for source, target in right]
    across = []
    for b in range(1, bands):
        for x in range(chips):
            here, there = b * chans + 2 * x + b % 2, (b - 1) * chans + 2 * x + b % 2
            across += [(here, there), (there, here)]
    for x in range(chips):
        here, there = 2 * x, (bands - 1) * chans + 2 * x + bands % 2
        across += [(here, there), (there, here)]

    def on_device(new_frames, cached_frames, conv_weight, out_bias):
        cols = new_frames.shape[-1]
        index = lax.axis_index("chan")
        core, chip = index % 2, index // 2
        even = core == 0
        flip = (core + lax.axis_index("band")) % 2
        upper = flip == 0
        band = lax.axis_index("band")
        edge = jnp.where(upper, band == 0, band == bands - 1)

        def send(a, pairs, axes="chan"):
            return lax.ppermute(a, axes, pairs)

        def halos(a, b):
            c = send(jnp.stack([a[1], b[1]]), swap)
            z = send(jnp.stack([a[0], b[0]]), across, ("band", "chan"))
            return (z[0], z[1]), (c[0], c[1])

        kept, sent = pack(flip.astype(jnp.int32).reshape(1), cached_frames, new_frames)
        got = send(sent, swap)
        got, conv_weight, out_bias = lax.optimization_barrier((got, conv_weight, out_bias))
        other_weight = send(conv_weight, swap)
        biases = jnp.stack([out_bias, send(out_bias, swap)])
        lo, hi = jnp.where(even, kept, got), jnp.where(even, got, kept)
        l_lo = send(lo, right)
        r_hi = send(hi, left)
        l_hi = send(hi, right)
        r_lo = send(lo, left)
        weights = (conv_weight, other_weight)

        def scalars(*offsets):
            first, second = (offsets * 2)[:2]
            return jnp.stack([flip, (chip + first) % chips, (chip + second) % chips, edge]).astype(jnp.int32)

        acc = block_call(scalars(0), (lo, hi), *halos(lo, hi), weights, False, None, None)
        l_lo, r_hi, acc = lax.optimization_barrier((l_lo, r_hi, acc))
        f_lo = send(l_lo, right)
        f_hi = send(r_hi, left)
        r_lo, l_hi, acc = lax.optimization_barrier((r_lo, l_hi, acc))
        acc = block_call(scalars(chips - 1, 1), (l_lo, r_hi), *halos(l_lo, r_hi), weights, True, acc, None)
        f_lo, f_hi, acc = lax.optimization_barrier((f_lo, f_hi, acc))
        acc = block_call(scalars(1, chips - 1), (r_lo, l_hi), *halos(r_lo, l_hi), weights, True, acc, None)
        mine, theirs = block_call(scalars(2), (f_lo, f_hi), *halos(f_lo, f_hi), weights, False, acc, biases)
        given = send(theirs, swap)

        def row(a, r):
            a = a[:, r]
            return jnp.stack([a[..., :cols], a[..., cols:]], axis=1).reshape(4, a.shape[1], cols)

        m, g = [row(mine, 0), row(mine, 1)], [row(given, 0), row(given, 1)]
        return jnp.stack([jnp.where(upper, a, b) for a, b in zip(m + g[::-1], g + m[::-1])], axis=1)

    in_specs = (
        P(None, "band", "chan", None),
        P(None, "band", "chan", None),
        P(None, None, None, "chan", None),
        P("chan"),
    )

    return jax.shard_map(
        on_device, mesh=mesh, in_specs=in_specs, out_specs=P(None, "band", "chan", None), check_vma=False
    )
```

```python
import functools

import jax
import jax.numpy as jnp
from jax import lax
from jax.experimental import pallas as pl
from jax.experimental.pallas import tpu as pltpu
from jax.sharding import PartitionSpec as P


BF = jnp.bfloat16
F32 = jnp.float32
LANES = 128
OWN, LEFT_RIGHT, RIGHT_LEFT, FAR = (2, 2), (3, 4), (4, 3), (5, 5)
HALF = 64


def turn(pairs):
    width = pairs.shape[-1]
    return pltpu.roll(pairs.astype(F32), width // 2, axis=1)


def pack_kernel(flip_ref, cached_ref, new_ref, kept_ref, sent_ref):
    cols = cached_ref.shape[-1]
    upper = flip_ref[0]
    place = [
        (lax.broadcasted_iota(jnp.int32, (cols, 2 * cols), 0) + h * cols
         == lax.broadcasted_iota(jnp.int32, (cols, 2 * cols), 1)).astype(F32).astype(BF)
        for h in range(2)
    ]
    for out, flip in ((kept_ref, upper), (sent_ref, 1 - upper)):
        for row in range(2):
            at = jnp.where(flip == 0, row, 3 - row)
            for pair in range(3):
                first = cached_ref[0, at] if pair == 0 else new_ref[2 * pair - 2, at]
                second = cached_ref[1, at] if pair == 0 else new_ref[2 * pair - 1, at]
                both = jnp.dot(first, place[0], preferred_element_type=F32)
                both = both + jnp.dot(second, place[1], preferred_element_type=F32)
                out[row, pair] = both.astype(BF)


def pack(flip, cached, new):
    channels, cols = cached.shape[2:]
    shape = jax.ShapeDtypeStruct((2, 3, channels, 2 * cols), BF)
    return pl.pallas_call(
        pack_kernel,
        in_specs=[pl.BlockSpec(memory_space=pltpu.SMEM)] + [pl.BlockSpec(memory_space=pltpu.VMEM)] * 2,
        out_specs=[pl.BlockSpec(memory_space=pltpu.VMEM)] * 2,
        out_shape=[shape, shape],
        compiler_params=pltpu.CompilerParams(vmem_limit_bytes=16 * 2**20),
        cost_estimate=pl.CostEstimate(flops=10**8, bytes_accessed=4 * 2**20, transcendentals=0),
        name="pack",
    )(flip, cached, new)


def block_kernel(blocks, first, last, *refs):
    scalars, refs = refs[0], list(refs[1:])
    bodies = [refs.pop(0), refs.pop(0)]
    zsides, csides = refs.pop(0), refs.pop(0)
    weights = [refs.pop(0), refs.pop(0)]
    before = None if first else refs.pop(0)
    bias = refs.pop(0) if last else None
    outs = [refs.pop(0), refs.pop(0)] if last else [refs.pop(0)]
    (xs,) = refs
    flip, edge = scalars[0], scalars[1] == 1
    width = xs.shape[-1]
    cols = width // 2
    near = lax.broadcasted_iota(jnp.int32, (HALF, width), 1) < cols
    lanes = [pl.ds(pl.multiple_of(scalars[at] * LANES, LANES), LANES) for at in blocks]
    mixed = blocks[0] != blocks[1]

    channel = lax.broadcasted_iota(jnp.int32, (1, LANES), 1)
    from_first = channel < HALF

    def one_pair(p, carry):
        for piece in range(2):
            at = pl.ds(piece * HALF, HALF)
            rows = [
                lambda q: jnp.where(edge, jnp.zeros((HALF, width), BF), zsides[piece, q]),
                lambda q: bodies[piece][0, q],
                lambda q: bodies[piece][1, q],
                lambda q: csides[piece, q],
            ]
            for row in range(4):
                low, high = rows[row](p), rows[row](p + 1)
                xs[0, row, at] = low
                xs[2, row, at] = high
                xs[1, row, at] = jnp.where(near, turn(low), turn(high)).astype(BF)

        taps = []
        for t in range(3):
            for delta in range(3):
                row_tap = jnp.where(flip == 0, delta, 2 - delta)
                halves = []
                for half in range(2):
                    w = weights[half][t, row_tap, :, :, lanes[0]]
                    w = w.reshape(w.shape[0] * w.shape[1], LANES)
                    if mixed:
                        v = weights[half][t, row_tap, :, :, lanes[1]].reshape(w.shape)
                        w = jnp.where(jnp.broadcast_to(from_first, w.shape), w, v)
                    halves.append(w)
                taps.append(jnp.concatenate(halves, axis=0))
        lhs = jnp.concatenate(taps, axis=1)
        rows = lhs.shape[0] // 6
        lane = lax.broadcasted_iota(jnp.int32, (rows, width), 1)
        zero = jnp.zeros((rows, width), F32)
        left_edge = (lane == 0) | (lane == cols)
        right_edge = (lane == cols - 1) | (lane == width - 1)
        for row in range(2):
            window = jnp.concatenate(
                [xs[t, row : row + 3].reshape(3 * LANES, width) for t in range(3)], axis=0
            )
            acc = jnp.dot(lhs, window, preferred_element_type=F32)
            if not first:
                acc = acc + before[p, row]
            if not last:
                outs[0][p, row] = acc
                continue
            for half in range(2):
                part = acc[half * 3 * rows : (half + 1) * 3 * rows]
                from_left = jnp.where(left_edge, zero, pltpu.roll(part[:rows], 1, axis=1))
                from_right = jnp.where(right_edge, zero, pltpu.roll(part[2 * rows :], width - 1, axis=1))
                total = part[rows : 2 * rows] + from_left + from_right + bias[half][:, None]
                outs[half][p, row] = total.astype(BF)
        return carry

    lax.fori_loop(0, 2, one_pair, 0)


def block_call(scalars, blocks, bodies, zsides, csides, weights, before, bias):
    first, last = before is None, bias is not None
    own, other = weights
    outs64 = own.shape[3]
    rows = 2 * 3 * outs64
    width = bodies[0].shape[-1]
    operands = [*bodies, zsides, csides, own, other]
    aliases = {}
    if not first:
        operands.append(before)
    if last:
        operands.append(bias)
        out_shape = [jax.ShapeDtypeStruct((2, 2, outs64, width), BF)] * 2
    else:
        out_shape = [jax.ShapeDtypeStruct((2, 2, rows, width), F32)]
        if not first:
            aliases = {len(operands): 0}
    vmem = pl.BlockSpec(memory_space=pltpu.VMEM)
    result = pl.pallas_call(
        functools.partial(block_kernel, blocks, first, last),
        in_specs=[pl.BlockSpec(memory_space=pltpu.SMEM)] + [vmem] * len(operands),
        out_specs=[vmem] * len(out_shape),
        scratch_shapes=[pltpu.VMEM((3, 4, LANES, width), BF)],
        out_shape=out_shape,
        input_output_aliases=aliases,
        compiler_params=pltpu.CompilerParams(vmem_limit_bytes=28 * 2**20),
        cost_estimate=pl.CostEstimate(
            flops=2 * 4 * rows * 9 * LANES * width, bytes_accessed=8 * 2**20, transcendentals=0
        ),
    )(scalars, *operands)
    return result if last else result[0]


def solution(mesh):
    bands, chans = mesh.shape["band"], mesh.shape["chan"]
    chips = chans // 2
    swap = [(2 * x + c, 2 * x + 1 - c) for x in range(chips) for c in range(2)]
    right = [(2 * x + c, 2 * ((x + 1) % chips) + c) for x in range(chips) for c in range(2)]
    left = [(target, source) for source, target in right]
    across = []
    for b in range(1, bands):
        for x in range(chips):
            here, there = b * chans + 2 * x + b % 2, (b - 1) * chans + 2 * x + b % 2
            across += [(here, there), (there, here)]
    for x in range(chips):
        for own in (2 * x, (bands - 1) * chans + 2 * x + bands % 2):
            across += [(own, own)]

    def on_device(new_frames, cached_frames, conv_weight, out_bias):
        cols = new_frames.shape[-1]
        index = lax.axis_index("chan")
        core, chip = index % 2, index // 2
        even = core == 0
        flip = (core + lax.axis_index("band")) % 2
        upper = flip == 0
        band = lax.axis_index("band")
        edge = jnp.where(upper, band == 0, band == bands - 1)

        def send(a, pairs, axes="chan"):
            return lax.ppermute(a, axes, pairs)

        def halos(a, b):
            c = send(jnp.stack([a[1], b[1]]), swap)
            z = send(jnp.stack([a[0], b[0]]), across, ("band", "chan"))
            return z, c

        scalars = jnp.stack([flip, edge.astype(flip.dtype)] + [(chip + o) % chips for o in (0, chips - 1, 1, 2)])
        scalars, upper, even = lax.optimization_barrier((scalars.astype(jnp.int32), upper, even))
        kept, sent = pack(scalars, cached_frames, new_frames)
        got = send(sent, swap)
        got, conv_weight, out_bias = lax.optimization_barrier((got, conv_weight, out_bias))
        other_weight = send(conv_weight, swap)
        biases = jnp.stack([out_bias, send(out_bias, swap)])
        lo, hi = jnp.where(even, kept, got), jnp.where(even, got, kept)
        l_lo = send(lo, right)
        r_hi = send(hi, left)
        l_hi = send(hi, right)
        r_lo = send(lo, left)
        weights = (conv_weight, other_weight)

        acc = block_call(scalars, OWN, (lo, hi), *halos(lo, hi), weights, None, None)
        l_lo, r_hi, acc = lax.optimization_barrier((l_lo, r_hi, acc))
        f_lo = send(l_lo, right)
        f_hi = send(r_hi, left)
        r_lo, l_hi, acc = lax.optimization_barrier((r_lo, l_hi, acc))
        acc = block_call(scalars, LEFT_RIGHT, (l_lo, r_hi), *halos(l_lo, r_hi), weights, acc, None)
        f_lo, f_hi, acc = lax.optimization_barrier((f_lo, f_hi, acc))
        acc = block_call(scalars, RIGHT_LEFT, (r_lo, l_hi), *halos(r_lo, l_hi), weights, acc, None)
        mine, theirs = block_call(scalars, FAR, (f_lo, f_hi), *halos(f_lo, f_hi), weights, acc, biases)
        given = send(theirs, swap)

        def row(a, r):
            a = a[:, r]
            return jnp.stack([a[..., :cols], a[..., cols:]], axis=1).reshape(4, a.shape[1], cols)

        m, g = [row(mine, 0), row(mine, 1)], [row(given, 0), row(given, 1)]
        return jnp.stack([jnp.where(upper, a, b) for a, b in zip(m + g[::-1], g + m[::-1])], axis=1)

    in_specs = (
        P(None, "band", "chan", None),
        P(None, "band", "chan", None),
        P(None, None, None, "chan", None),
        P("chan"),
    )

    return jax.shard_map(
        on_device, mesh=mesh, in_specs=in_specs, out_specs=P(None, "band", "chan", None), check_vma=False
    )
```

```python
import functools

import jax
import jax.numpy as jnp
from jax import lax
from jax.experimental import pallas as pl
from jax.experimental.pallas import tpu as pltpu
from jax.sharding import PartitionSpec as P


BF = jnp.bfloat16
F32 = jnp.float32
LANES = 128
OWN, LEFT_RIGHT, RIGHT_LEFT, FAR = (2, 2), (3, 4), (4, 3), (5, 5)
HALF = 64


def turn(pairs):
    width = pairs.shape[-1]
    return pltpu.roll(pairs.astype(F32), width // 2, axis=1)


def pack_kernel(flip_ref, cached_ref, new_ref, kept_ref, sent_ref):
    cols = cached_ref.shape[-1]
    upper = flip_ref[0]
    place = [
        (lax.broadcasted_iota(jnp.int32, (cols, 2 * cols), 0) + h * cols
         == lax.broadcasted_iota(jnp.int32, (cols, 2 * cols), 1)).astype(F32).astype(BF)
        for h in range(2)
    ]
    for out, flip in ((kept_ref, upper), (sent_ref, 1 - upper)):
        for row in range(2):
            at = jnp.where(flip == 0, row, 3 - row)
            for pair in range(3):
                first = cached_ref[0, at] if pair == 0 else new_ref[2 * pair - 2, at]
                second = cached_ref[1, at] if pair == 0 else new_ref[2 * pair - 1, at]
                both = jnp.dot(first, place[0], preferred_element_type=F32)
                both = both + jnp.dot(second, place[1], preferred_element_type=F32)
                out[row, pair] = both.astype(BF)


def pack(flip, cached, new):
    channels, cols = cached.shape[2:]
    shape = jax.ShapeDtypeStruct((2, 3, channels, 2 * cols), BF)
    return pl.pallas_call(
        pack_kernel,
        in_specs=[pl.BlockSpec(memory_space=pltpu.SMEM)] + [pl.BlockSpec(memory_space=pltpu.VMEM)] * 2,
        out_specs=[pl.BlockSpec(memory_space=pltpu.VMEM)] * 2,
        out_shape=[shape, shape],
        compiler_params=pltpu.CompilerParams(vmem_limit_bytes=16 * 2**20),
        cost_estimate=pl.CostEstimate(flops=10**8, bytes_accessed=4 * 2**20, transcendentals=0),
        name="pack",
    )(flip, cached, new)


def block_kernel(blocks, part, first, last, *refs):
    scalars, refs = refs[0], list(refs[1:])
    bodies = None if part == "z" else [refs.pop(0), refs.pop(0)]
    zsides = None if part == "main" else refs.pop(0)
    csides = None if part == "z" else refs.pop(0)
    held = {"all": range(4), "main": range(1, 4), "z": range(1)}[part]
    weights = [refs.pop(0), refs.pop(0)]
    before = None if first else refs.pop(0)
    bias = refs.pop(0) if last else None
    outs = [refs.pop(0), refs.pop(0)] if last else [refs.pop(0)]
    (xs,) = refs
    flip, edge = scalars[0], scalars[1] == 1
    width = xs.shape[-1]
    cols = width // 2
    near = lax.broadcasted_iota(jnp.int32, (HALF, width), 1) < cols
    lanes = [pl.ds(pl.multiple_of(scalars[at] * LANES, LANES), LANES) for at in blocks]
    mixed = blocks[0] != blocks[1]

    channel = lax.broadcasted_iota(jnp.int32, (1, LANES), 1)
    from_first = channel < HALF

    def one_pair(p, carry):
        for piece in range(2):
            at = pl.ds(piece * HALF, HALF)
            rows = [
                lambda q: jnp.where(edge, jnp.zeros((HALF, width), BF), zsides[piece, q]),
                lambda q: bodies[piece][0, q],
                lambda q: bodies[piece][1, q],
                lambda q: csides[piece, q],
            ]
            for row in held:
                low, high = rows[row](p), rows[row](p + 1)
                xs[0, row, at] = low
                xs[2, row, at] = high
                xs[1, row, at] = jnp.where(near, turn(low), turn(high)).astype(BF)

        taps = []
        for t in range(3):
            for delta in range(3):
                row_tap = jnp.where(flip == 0, delta, 2 - delta)
                halves = []
                for half in range(2):
                    w = weights[half][t, row_tap, :, :, lanes[0]]
                    w = w.reshape(w.shape[0] * w.shape[1], LANES)
                    if mixed:
                        v = weights[half][t, row_tap, :, :, lanes[1]].reshape(w.shape)
                        w = jnp.where(jnp.broadcast_to(from_first, w.shape), w, v)
                    halves.append(w)
                taps.append(jnp.concatenate(halves, axis=0))
        rows = taps[0].shape[0] // 6
        lane = lax.broadcasted_iota(jnp.int32, (rows, width), 1)
        zero = jnp.zeros((rows, width), F32)
        left_edge = (lane == 0) | (lane == cols)
        right_edge = (lane == cols - 1) | (lane == width - 1)
        for row in range(2):
            acc = None if first else before[p, row]
            at = [(t, delta) for t in range(3) for delta in range(3) if row + delta in held]
            if at:
                lhs = jnp.concatenate([taps[3 * t + delta] for t, delta in at], axis=1)
                window = jnp.concatenate([xs[t, row + delta] for t, delta in at], axis=0)
                product = jnp.dot(lhs, window, preferred_element_type=F32)
                acc = product if first else acc + product
            if not last:
                outs[0][p, row] = acc
                continue
            for half in range(2):
                part = acc[half * 3 * rows : (half + 1) * 3 * rows]
                from_left = jnp.where(left_edge, zero, pltpu.roll(part[:rows], 1, axis=1))
                from_right = jnp.where(right_edge, zero, pltpu.roll(part[2 * rows :], width - 1, axis=1))
                total = part[rows : 2 * rows] + from_left + from_right + bias[half][:, None]
                outs[half][p, row] = total.astype(BF)
        return carry

    lax.fori_loop(0, 2, one_pair, 0)


def block_call(scalars, blocks, part, bodies, zsides, csides, weights, before, bias):
    first, last = before is None, bias is not None
    own, other = weights
    outs64 = own.shape[3]
    rows = 2 * 3 * outs64
    width = (bodies[0] if part != "z" else zsides).shape[-1]
    operands = [own, other]
    if part != "z":
        operands.insert(0, csides)
    if part != "main":
        operands.insert(0, zsides)
    if part != "z":
        operands = [*bodies, *operands]
    aliases = {}
    if not first:
        operands.append(before)
    if last:
        operands.append(bias)
        out_shape = [jax.ShapeDtypeStruct((2, 2, outs64, width), BF)] * 2
    else:
        out_shape = [jax.ShapeDtypeStruct((2, 2, rows, width), F32)]
        if not first:
            aliases = {len(operands): 0}
    vmem = pl.BlockSpec(memory_space=pltpu.VMEM)
    result = pl.pallas_call(
        functools.partial(block_kernel, blocks, part, first, last),
        in_specs=[pl.BlockSpec(memory_space=pltpu.SMEM)] + [vmem] * len(operands),
        out_specs=[vmem] * len(out_shape),
        scratch_shapes=[pltpu.VMEM((3, 4, LANES, width), BF)],
        out_shape=out_shape,
        input_output_aliases=aliases,
        compiler_params=pltpu.CompilerParams(vmem_limit_bytes=28 * 2**20),
        cost_estimate=pl.CostEstimate(
            flops=2 * 4 * rows * 9 * LANES * width, bytes_accessed=8 * 2**20, transcendentals=0
        ),
    )(scalars, *operands)
    return result if last else result[0]


def solution(mesh):
    bands, chans = mesh.shape["band"], mesh.shape["chan"]
    chips = chans // 2
    swap = [(2 * x + c, 2 * x + 1 - c) for x in range(chips) for c in range(2)]
    right = [(2 * x + c, 2 * ((x + 1) % chips) + c) for x in range(chips) for c in range(2)]
    left = [(target, source) for source, target in right]
    across = []
    for b in range(1, bands):
        for x in range(chips):
            here, there = b * chans + 2 * x + b % 2, (b - 1) * chans + 2 * x + b % 2
            across += [(here, there), (there, here)]
    for x in range(chips):
        here, there = 2 * x, (bands - 1) * chans + 2 * x + bands % 2
        across += [(here, there), (there, here)]

    def on_device(new_frames, cached_frames, conv_weight, out_bias):
        cols = new_frames.shape[-1]
        index = lax.axis_index("chan")
        core, chip = index % 2, index // 2
        even = core == 0
        flip = (core + lax.axis_index("band")) % 2
        upper = flip == 0
        band = lax.axis_index("band")
        edge = jnp.where(upper, band == 0, band == bands - 1)

        def send(a, pairs, axes="chan"):
            return lax.ppermute(a, axes, pairs)

        def halos(a, b):
            c = send(jnp.stack([a[1], b[1]]), swap)
            z = send(jnp.stack([a[0], b[0]]), across, ("band", "chan"))
            return z, c

        scalars = jnp.stack([flip, edge.astype(flip.dtype)] + [(chip + o) % chips for o in (0, chips - 1, 1, 2)])
        scalars, upper, even = lax.optimization_barrier((scalars.astype(jnp.int32), upper, even))
        kept, sent = pack(scalars, cached_frames, new_frames)
        got = send(sent, swap)
        got, conv_weight, out_bias = lax.optimization_barrier((got, conv_weight, out_bias))
        other_weight = send(conv_weight, swap)
        biases = jnp.stack([out_bias, send(out_bias, swap)])
        lo, hi = jnp.where(even, kept, got), jnp.where(even, got, kept)
        l_lo = send(lo, right)
        r_hi = send(hi, left)
        l_hi = send(hi, right)
        r_lo = send(lo, left)
        weights = (conv_weight, other_weight)

        acc = block_call(scalars, OWN, "all", (lo, hi), *halos(lo, hi), weights, None, None)
        f_lo = send(l_lo, right)
        f_hi = send(r_hi, left)
        acc = block_call(scalars, LEFT_RIGHT, "all", (l_lo, r_hi), *halos(l_lo, r_hi), weights, acc, None)
        acc = block_call(scalars, RIGHT_LEFT, "all", (r_lo, l_hi), *halos(r_lo, l_hi), weights, acc, None)
        far_z, far_c = halos(f_lo, f_hi)
        acc = block_call(scalars, FAR, "main", (f_lo, f_hi), None, far_c, weights, acc, None)
        mine, theirs = block_call(scalars, FAR, "z", None, far_z, None, weights, acc, biases)
        given = send(theirs, swap)

        def row(a, r):
            a = a[:, r]
            return jnp.stack([a[..., :cols], a[..., cols:]], axis=1).reshape(4, a.shape[1], cols)

        m, g = [row(mine, 0), row(mine, 1)], [row(given, 0), row(given, 1)]
        return jnp.stack([jnp.where(upper, a, b) for a, b in zip(m + g[::-1], g + m[::-1])], axis=1)

    in_specs = (
        P(None, "band", "chan", None),
        P(None, "band", "chan", None),
        P(None, None, None, "chan", None),
        P("chan"),
    )

    return jax.shard_map(
        on_device, mesh=mesh, in_specs=in_specs, out_specs=P(None, "band", "chan", None), check_vma=False
    )
```

```python
import functools

import jax
import jax.numpy as jnp
from jax import lax
from jax.experimental import pallas as pl
from jax.experimental.pallas import tpu as pltpu
from jax.sharding import PartitionSpec as P


BF = jnp.bfloat16
F32 = jnp.float32
LANES = 128
OWN, LEFT_RIGHT, RIGHT_LEFT, FAR = (2, 2), (3, 4), (4, 3), (5, 5)
HALF = 64


def turn(pairs):
    width = pairs.shape[-1]
    return pltpu.roll(pairs.astype(F32), width // 2, axis=1)


def pack_kernel(flip_ref, cached_ref, new_ref, kept_ref, sent_ref):
    cols = cached_ref.shape[-1]
    upper = flip_ref[0]
    place = [
        (lax.broadcasted_iota(jnp.int32, (cols, 2 * cols), 0) + h * cols
         == lax.broadcasted_iota(jnp.int32, (cols, 2 * cols), 1)).astype(F32).astype(BF)
        for h in range(2)
    ]
    for out, flip in ((kept_ref, upper), (sent_ref, 1 - upper)):
        for row in range(2):
            at = jnp.where(flip == 0, row, 3 - row)
            channels = cached_ref.shape[2]
            firsts = jnp.concatenate([cached_ref[0, at], new_ref[0, at], new_ref[2, at]], axis=0)
            seconds = jnp.concatenate([cached_ref[1, at], new_ref[1, at], new_ref[3, at]], axis=0)
            both = jnp.dot(firsts, place[0], preferred_element_type=F32)
            both = both + jnp.dot(seconds, place[1], preferred_element_type=F32)
            out[row] = both.astype(BF).reshape(3, channels, 2 * cols)


def pack(flip, cached, new):
    channels, cols = cached.shape[2:]
    shape = jax.ShapeDtypeStruct((2, 3, channels, 2 * cols), BF)
    return pl.pallas_call(
        pack_kernel,
        in_specs=[pl.BlockSpec(memory_space=pltpu.SMEM)] + [pl.BlockSpec(memory_space=pltpu.VMEM)] * 2,
        out_specs=[pl.BlockSpec(memory_space=pltpu.VMEM)] * 2,
        out_shape=[shape, shape],
        compiler_params=pltpu.CompilerParams(vmem_limit_bytes=16 * 2**20),
        cost_estimate=pl.CostEstimate(flops=10**8, bytes_accessed=4 * 2**20, transcendentals=0),
        name="pack",
    )(flip, cached, new)


def unpack_kernel(scalars, *refs):
    rows, (out, turned, sems) = refs[:4], refs[4:]
    cols = turned.shape[-1]
    copies = []
    for at, source in enumerate(rows):
        inner = at % 2
        lower = scalars[0] if at < 2 else 1 - scalars[0]
        row = jnp.where(lower == 0, inner, 3 - inner)
        for p in range(2):
            pair = source[p]
            turned[at, 2 * p] = pair[:, :cols]
            turned[at, 2 * p + 1] = turn(pair).astype(BF)[:, :cols]
            both = pl.ds(2 * p, 2)
            copies.append(pltpu.make_async_copy(turned.at[at, both], out.at[both, row], sems.at[at, p]))
            copies[-1].start()
    for copy in copies:
        copy.wait()


def unpack(scalars, rows, shape):
    vmem = pl.BlockSpec(memory_space=pltpu.VMEM)
    return pl.pallas_call(
        unpack_kernel,
        in_specs=[pl.BlockSpec(memory_space=pltpu.SMEM)] + [vmem] * 4,
        out_specs=pl.BlockSpec(memory_space=pltpu.HBM),
        out_shape=jax.ShapeDtypeStruct(shape, BF),
        scratch_shapes=[pltpu.VMEM((4, 4, *shape[2:]), BF), pltpu.SemaphoreType.DMA((4, 2))],
        compiler_params=pltpu.CompilerParams(vmem_limit_bytes=16 * 2**20),
        cost_estimate=pl.CostEstimate(flops=10**7, bytes_accessed=4 * 2**20, transcendentals=0),
        name="unpack",
    )(scalars, *rows)


def column_sum(acc, bias, cols):
    rows, width = acc.shape[0] // 6, acc.shape[1]
    lane = lax.broadcasted_iota(jnp.int32, (rows, width), 1)
    zero = jnp.zeros((rows, width), F32)
    left_edge = (lane == 0) | (lane == cols)
    right_edge = (lane == cols - 1) | (lane == width - 1)
    totals = []
    for half in range(2):
        part = acc[half * 3 * rows : (half + 1) * 3 * rows]
        from_left = jnp.where(left_edge, zero, pltpu.roll(part[:rows], 1, axis=1))
        from_right = jnp.where(right_edge, zero, pltpu.roll(part[2 * rows :], width - 1, axis=1))
        totals.append((part[rows : 2 * rows] + from_left + from_right + bias[half][:, None]).astype(BF))
    return totals


def tap_weights(scalars, blocks, weights, t, delta):
    lanes = [pl.ds(pl.multiple_of(scalars[at] * LANES, LANES), LANES) for at in blocks]
    row_tap = jnp.where(scalars[0] == 0, delta, 2 - delta)
    halves = []
    for half in range(2):
        w = weights[half][t, row_tap, :, :, lanes[0]]
        w = w.reshape(w.shape[0] * w.shape[1], LANES)
        if blocks[0] != blocks[1]:
            v = weights[half][t, row_tap, :, :, lanes[1]].reshape(w.shape)
            first = lax.broadcasted_iota(jnp.int32, (1, LANES), 1) < HALF
            w = jnp.where(jnp.broadcast_to(first, w.shape), w, v)
        halves.append(w)
    return jnp.concatenate(halves, axis=0)


def put_pairs(xs, at, low, high):
    near = lax.broadcasted_iota(jnp.int32, low.shape, 1) < low.shape[1] // 2
    xs[(0, *at)] = low
    xs[(2, *at)] = high
    xs[(1, *at)] = jnp.where(near, turn(low), turn(high)).astype(BF)


def main_kernel(blocks, first, last, *refs):
    scalars, lo, hi, csides, own, other, *refs = refs
    before = None if first else refs.pop(0)
    bias = refs.pop(0) if last else None
    xs = refs.pop()
    cols = xs.shape[-1] // 2

    def one_pair(p, carry):
        for piece, body in enumerate((lo, hi)):
            at = pl.ds(piece * HALF, HALF)
            for row in range(3):
                low, high = ((body[row, p], body[row, p + 1]) if row < 2 else (csides[piece, p], csides[piece, p + 1]))
                put_pairs(xs, (row, at), low, high)
        taps = {
            (t, delta): tap_weights(scalars, blocks, (own, other), t, delta) for t in range(3) for delta in range(3)
        }
        for row in range(2):
            used = [at for at in taps if row + at[1] >= 1]
            lhs = jnp.concatenate([taps[at] for at in used], axis=1)
            window = jnp.concatenate([xs[t, row + delta - 1] for t, delta in used], axis=0)
            acc = jnp.dot(lhs, window, preferred_element_type=F32)
            if not first:
                acc = acc + before[p, row]
            if not last:
                refs[0][p, row] = acc
            elif row == 0:
                refs[0][p] = acc
            else:
                refs[1][p], refs[2][p] = column_sum(acc, bias, cols)
        return carry

    lax.fori_loop(0, 2, one_pair, 0)


def z_kernel(sources, last, *refs):
    scalars, *refs = refs
    zs = [refs.pop(0) for _ in range(1 + max(which for _, which, _ in sources))]
    own, other, before = refs[:3]
    refs = refs[3:]
    bias = refs.pop(0) if last else None
    xs = refs.pop()
    width = xs.shape[-1]
    edge = scalars[1] == 1

    def one_pair(p, carry):
        lhs, window = [], []
        for slot, (blocks, which, start) in enumerate(sources):
            for piece in range(2):
                low, high = (
                    jnp.where(edge, jnp.zeros((HALF, width), BF), zs[which][start + piece, q]) for q in (p, p + 1)
                )
                put_pairs(xs, (slot, pl.ds(piece * HALF, HALF)), low, high)
            for t in range(3):
                lhs.append(tap_weights(scalars, blocks, (own, other), t, 0))
                window.append(xs[t, slot])
        acc = before[p] + jnp.dot(
            jnp.concatenate(lhs, axis=1), jnp.concatenate(window, axis=0), preferred_element_type=F32
        )
        if last:
            refs[0][p], refs[1][p] = column_sum(acc, bias, width // 2)
        else:
            refs[0][p] = acc
        return carry

    lax.fori_loop(0, 2, one_pair, 0)


def kernel_call(body, scalars, operands, out_shape, aliases, scratch, flops):
    vmem = pl.BlockSpec(memory_space=pltpu.VMEM)
    return pl.pallas_call(
        body,
        in_specs=[pl.BlockSpec(memory_space=pltpu.SMEM)] + [vmem] * len(operands),
        out_specs=[vmem] * len(out_shape),
        scratch_shapes=[pltpu.VMEM(scratch, BF)],
        out_shape=out_shape,
        input_output_aliases=aliases,
        compiler_params=pltpu.CompilerParams(vmem_limit_bytes=28 * 2**20),
        cost_estimate=pl.CostEstimate(flops=flops, bytes_accessed=8 * 2**20, transcendentals=0),
    )(scalars, *operands)


def main_call(scalars, blocks, bodies, csides, weights, before, bias):
    first, last = before is None, bias is not None
    outs, width = weights[0].shape[3], csides.shape[-1]
    operands = [*bodies, csides, *weights]
    aliases = {}
    if last:
        operands += [before, bias]
        out_shape = [jax.ShapeDtypeStruct((2, 6 * outs, width), F32)] + [jax.ShapeDtypeStruct((2, outs, width), BF)] * 2
    else:
        out_shape = [jax.ShapeDtypeStruct((2, 2, 6 * outs, width), F32)]
        if not first:
            operands.append(before)
            aliases = {len(operands): 0}
    result = kernel_call(
        functools.partial(main_kernel, blocks, first, last), scalars, operands, out_shape, aliases,
        (3, 3, LANES, width), 2 * 6 * outs * 30 * LANES * width,
    )
    return result if last else result[0]


def z_call(scalars, sources, zs, weights, before, bias):
    last = bias is not None
    outs, width = weights[0].shape[3], before.shape[-1]
    operands = [*zs, *weights, before]
    aliases = {}
    if last:
        operands.append(bias)
        out_shape = [jax.ShapeDtypeStruct((2, outs, width), BF)] * 2
    else:
        out_shape = [jax.ShapeDtypeStruct((2, 6 * outs, width), F32)]
        aliases = {len(operands): 0}
    result = kernel_call(
        functools.partial(z_kernel, sources, last), scalars, operands, out_shape, aliases,
        (3, len(sources), LANES, width), 2 * 6 * outs * 6 * len(sources) * LANES * width,
    )
    return result if last else result[0]


def solution(mesh):
    bands, chans = mesh.shape["band"], mesh.shape["chan"]
    chips = chans // 2
    swap = [(2 * x + c, 2 * x + 1 - c) for x in range(chips) for c in range(2)]
    right = [(2 * x + c, 2 * ((x + 1) % chips) + c) for x in range(chips) for c in range(2)]
    left = [(target, source) for source, target in right]
    across = []
    for b in range(1, bands):
        for x in range(chips):
            here, there = b * chans + 2 * x + b % 2, (b - 1) * chans + 2 * x + b % 2
            across += [(here, there), (there, here)]
    for x in range(chips):
        here, there = 2 * x, (bands - 1) * chans + 2 * x + bands % 2
        across += [(here, there), (there, here)]

    def on_device(new_frames, cached_frames, conv_weight, out_bias):
        index = lax.axis_index("chan")
        core, chip = index % 2, index // 2
        even = core == 0
        flip = (core + lax.axis_index("band")) % 2
        upper = flip == 0
        band = lax.axis_index("band")
        edge = jnp.where(upper, band == 0, band == bands - 1)

        def send(a, pairs, axes="chan"):
            return lax.ppermute(a, axes, pairs)

        def other_core(*pieces):
            return send(jnp.stack([piece[1] for piece in pieces]), swap)

        def next_band(*pieces):
            return send(jnp.stack([piece[0] for piece in pieces]), across, ("band", "chan"))

        scalars = jnp.stack([flip, edge.astype(flip.dtype)] + [(chip + o) % chips for o in (0, chips - 1, 1, 2)])
        scalars, upper, even = lax.optimization_barrier((scalars.astype(jnp.int32), upper, even))
        kept, sent = pack(scalars, cached_frames, new_frames)
        got = send(sent, swap)
        got, conv_weight, out_bias = lax.optimization_barrier((got, conv_weight, out_bias))
        other_weight = send(conv_weight, swap)
        biases = jnp.stack([out_bias, send(out_bias, swap)])
        biases, scalars = lax.optimization_barrier((biases, scalars))
        lo, hi = jnp.where(even, kept, got), jnp.where(even, got, kept)
        l_lo = send(lo, right)
        r_hi = send(hi, left)
        l_hi = send(hi, right)
        r_lo = send(lo, left)
        weights = (conv_weight, other_weight)

        z_own = next_band(lo, hi)
        acc = main_call(scalars, OWN, (lo, hi), other_core(lo, hi), weights, None, None)
        f_lo = send(l_lo, right)
        f_hi = send(r_hi, left)
        acc = main_call(scalars, LEFT_RIGHT, (l_lo, r_hi), other_core(l_lo, r_hi), weights, acc, None)
        z_sides = next_band(l_lo, r_hi, r_lo, l_hi)
        acc = main_call(scalars, RIGHT_LEFT, (r_lo, l_hi), other_core(r_lo, l_hi), weights, acc, None)
        z_far = next_band(f_lo, f_hi)
        acc, inner, inner_theirs = main_call(scalars, FAR, (f_lo, f_hi), other_core(f_lo, f_hi), weights, acc, biases)
        inner_given = send(inner_theirs, swap)
        sources = ((OWN, 0, 0), (LEFT_RIGHT, 1, 0), (RIGHT_LEFT, 1, 2))
        acc = z_call(scalars, sources, (z_own, z_sides), weights, acc, None)
        outer, outer_theirs = z_call(scalars, ((FAR, 0, 0),), (z_far,), weights, acc, biases)
        outer_given = send(outer_theirs, swap)
        return unpack(scalars, (outer, inner, outer_given, inner_given), new_frames.shape)

    in_specs = (
        P(None, "band", "chan", None),
        P(None, "band", "chan", None),
        P(None, None, None, "chan", None),
        P("chan"),
    )

    return jax.shard_map(
        on_device, mesh=mesh, in_specs=in_specs, out_specs=P(None, "band", "chan", None), check_vma=False
    )
```

```python
import functools

import jax
import jax.numpy as jnp
from jax import lax
from jax.experimental import pallas as pl
from jax.experimental.pallas import tpu as pltpu
from jax.sharding import PartitionSpec as P


BF = jnp.bfloat16
F32 = jnp.float32
LANES = 128
OWN, LEFT_RIGHT, RIGHT_LEFT, FAR = (2, 2), (3, 4), (4, 3), (5, 5)
HALF = 64


def turn(pairs):
    width = pairs.shape[-1]
    return pltpu.roll(pairs.astype(F32), width // 2, axis=1)


def pack_kernel(flip_ref, cached_ref, new_ref, kept_ref, sent_ref):
    cols = cached_ref.shape[-1]
    upper = flip_ref[0]
    place = [
        (lax.broadcasted_iota(jnp.int32, (cols, 2 * cols), 0) + h * cols
         == lax.broadcasted_iota(jnp.int32, (cols, 2 * cols), 1)).astype(F32).astype(BF)
        for h in range(2)
    ]
    for out, flip in ((kept_ref, upper), (sent_ref, 1 - upper)):
        for row in range(2):
            at = jnp.where(flip == 0, row, 3 - row)
            channels = cached_ref.shape[2]
            firsts = jnp.concatenate([cached_ref[0, at], new_ref[0, at], new_ref[2, at]], axis=0)
            seconds = jnp.concatenate([cached_ref[1, at], new_ref[1, at], new_ref[3, at]], axis=0)
            both = jnp.dot(firsts, place[0], preferred_element_type=F32)
            both = both + jnp.dot(seconds, place[1], preferred_element_type=F32)
            out[row] = both.astype(BF).reshape(3, channels, 2 * cols)


def pack(flip, cached, new):
    channels, cols = cached.shape[2:]
    shape = jax.ShapeDtypeStruct((2, 3, channels, 2 * cols), BF)
    return pl.pallas_call(
        pack_kernel,
        in_specs=[pl.BlockSpec(memory_space=pltpu.SMEM)] + [pl.BlockSpec(memory_space=pltpu.VMEM)] * 2,
        out_specs=[pl.BlockSpec(memory_space=pltpu.VMEM)] * 2,
        out_shape=[shape, shape],
        compiler_params=pltpu.CompilerParams(vmem_limit_bytes=16 * 2**20),
        cost_estimate=pl.CostEstimate(flops=10**8, bytes_accessed=4 * 2**20, transcendentals=0),
        name="pack",
    )(flip, cached, new)


def unpack_kernel(scalars, *refs):
    rows, (out, turned, sems) = refs[:4], refs[4:]
    cols = turned.shape[-1]
    copies = []
    for at, source in enumerate(rows):
        inner = at % 2
        lower = scalars[0] if at < 2 else 1 - scalars[0]
        row = jnp.where(lower == 0, inner, 3 - inner)
        for p in range(2):
            pair = source[p]
            turned[at, 2 * p] = pair[:, :cols]
            turned[at, 2 * p + 1] = turn(pair).astype(BF)[:, :cols]
            both = pl.ds(2 * p, 2)
            copies.append(pltpu.make_async_copy(turned.at[at, both], out.at[both, row], sems.at[at, p]))
            copies[-1].start()
    for copy in copies:
        copy.wait()


def unpack(scalars, rows, shape):
    vmem = pl.BlockSpec(memory_space=pltpu.VMEM)
    return pl.pallas_call(
        unpack_kernel,
        in_specs=[pl.BlockSpec(memory_space=pltpu.SMEM)] + [vmem] * 4,
        out_specs=pl.BlockSpec(memory_space=pltpu.HBM),
        out_shape=jax.ShapeDtypeStruct(shape, BF),
        scratch_shapes=[pltpu.VMEM((4, 4, *shape[2:]), BF), pltpu.SemaphoreType.DMA((4, 2))],
        compiler_params=pltpu.CompilerParams(vmem_limit_bytes=16 * 2**20),
        cost_estimate=pl.CostEstimate(flops=10**7, bytes_accessed=4 * 2**20, transcendentals=0),
        name="unpack",
    )(scalars, *rows)


def column_sum(acc, bias, cols):
    rows, width = acc.shape[0] // 6, acc.shape[1]
    lane = lax.broadcasted_iota(jnp.int32, (rows, width), 1)
    zero = jnp.zeros((rows, width), F32)
    left_edge = (lane == 0) | (lane == cols)
    right_edge = (lane == cols - 1) | (lane == width - 1)
    totals = []
    for half in range(2):
        part = acc[half * 3 * rows : (half + 1) * 3 * rows]
        from_left = jnp.where(left_edge, zero, pltpu.roll(part[:rows], 1, axis=1))
        from_right = jnp.where(right_edge, zero, pltpu.roll(part[2 * rows :], width - 1, axis=1))
        totals.append((part[rows : 2 * rows] + from_left + from_right + bias[half][:, None]).astype(BF))
    return totals


def tap_weights(scalars, blocks, weights, t, delta):
    lanes = [pl.ds(pl.multiple_of(scalars[at] * LANES, LANES), LANES) for at in blocks]
    row_tap = jnp.where(scalars[0] == 0, delta, 2 - delta)
    halves = []
    for half in range(2):
        w = weights[half][t, row_tap, :, :, lanes[0]]
        w = w.reshape(w.shape[0] * w.shape[1], LANES)
        if blocks[0] != blocks[1]:
            v = weights[half][t, row_tap, :, :, lanes[1]].reshape(w.shape)
            first = lax.broadcasted_iota(jnp.int32, (1, LANES), 1) < HALF
            w = jnp.where(jnp.broadcast_to(first, w.shape), w, v)
        halves.append(w)
    return jnp.concatenate(halves, axis=0)


def put_pairs(xs, at, low, high):
    near = lax.broadcasted_iota(jnp.int32, low.shape, 1) < low.shape[1] // 2
    xs[(0, *at)] = low
    xs[(2, *at)] = high
    xs[(1, *at)] = jnp.where(near, turn(low), turn(high)).astype(BF)


def main_kernel(blocks, first, last, *refs):
    scalars, lo, hi, csides, own, other, *refs = refs
    before = None if first else refs.pop(0)
    bias = refs.pop(0) if last else None
    xs = refs.pop()
    cols = xs.shape[-1] // 2

    def one_pair(p, carry):
        for piece, body in enumerate((lo, hi)):
            at = pl.ds(piece * HALF, HALF)
            for row in range(3):
                low, high = ((body[row, p], body[row, p + 1]) if row < 2 else (csides[piece, p], csides[piece, p + 1]))
                put_pairs(xs, (row, at), low, high)
        taps = {
            (t, delta): tap_weights(scalars, blocks, (own, other), t, delta) for t in range(3) for delta in range(3)
        }
        for row in range(2):
            used = [at for at in taps if row + at[1] >= 1]
            lhs = jnp.concatenate([taps[at] for at in used], axis=1)
            window = jnp.concatenate([xs[t, row + delta - 1] for t, delta in used], axis=0)
            acc = jnp.dot(lhs, window, preferred_element_type=F32)
            if not first:
                acc = acc + before[p, row]
            if not last:
                refs[0][p, row] = acc
            elif row == 0:
                refs[0][p] = acc
            else:
                refs[1][p], refs[2][p] = column_sum(acc, bias, cols)
        return carry

    lax.fori_loop(0, 2, one_pair, 0)


def z_kernel(sources, last, *refs):
    scalars, *refs = refs
    zs = [refs.pop(0) for _ in range(1 + max(which for _, which, _ in sources))]
    own, other, before = refs[:3]
    refs = refs[3:]
    bias = refs.pop(0) if last else None
    xs = refs.pop()
    width = xs.shape[-1]
    edge = scalars[1] == 1

    def one_pair(p, carry):
        lhs, window = [], []
        for slot, (blocks, which, start) in enumerate(sources):
            for piece in range(2):
                low, high = (
                    jnp.where(edge, jnp.zeros((HALF, width), BF), zs[which][start + piece, q]) for q in (p, p + 1)
                )
                put_pairs(xs, (slot, pl.ds(piece * HALF, HALF)), low, high)
            for t in range(3):
                lhs.append(tap_weights(scalars, blocks, (own, other), t, 0))
                window.append(xs[t, slot])
        acc = before[p] + jnp.dot(
            jnp.concatenate(lhs, axis=1), jnp.concatenate(window, axis=0), preferred_element_type=F32
        )
        if last:
            refs[0][p], refs[1][p] = column_sum(acc, bias, width // 2)
        else:
            refs[0][p] = acc
        return carry

    lax.fori_loop(0, 2, one_pair, 0)


def kernel_call(body, scalars, operands, out_shape, aliases, scratch, flops):
    vmem = pl.BlockSpec(memory_space=pltpu.VMEM)
    return pl.pallas_call(
        body,
        in_specs=[pl.BlockSpec(memory_space=pltpu.SMEM)] + [vmem] * len(operands),
        out_specs=[vmem] * len(out_shape),
        scratch_shapes=[pltpu.VMEM(scratch, BF)],
        out_shape=out_shape,
        input_output_aliases=aliases,
        compiler_params=pltpu.CompilerParams(vmem_limit_bytes=28 * 2**20),
        cost_estimate=pl.CostEstimate(flops=flops, bytes_accessed=8 * 2**20, transcendentals=0),
    )(scalars, *operands)


def main_call(scalars, blocks, bodies, csides, weights, before, bias):
    first, last = before is None, bias is not None
    outs, width = weights[0].shape[3], csides.shape[-1]
    operands = [*bodies, csides, *weights]
    aliases = {}
    if last:
        operands += [before, bias]
        out_shape = [jax.ShapeDtypeStruct((2, 6 * outs, width), F32)] + [jax.ShapeDtypeStruct((2, outs, width), BF)] * 2
    else:
        out_shape = [jax.ShapeDtypeStruct((2, 2, 6 * outs, width), F32)]
        if not first:
            operands.append(before)
            aliases = {len(operands): 0}
    result = kernel_call(
        functools.partial(main_kernel, blocks, first, last), scalars, operands, out_shape, aliases,
        (3, 3, LANES, width), 2 * 6 * outs * 30 * LANES * width,
    )
    return result if last else result[0]


def z_call(scalars, sources, zs, weights, before, bias):
    last = bias is not None
    outs, width = weights[0].shape[3], before.shape[-1]
    operands = [*zs, *weights, before]
    aliases = {}
    if last:
        operands.append(bias)
        out_shape = [jax.ShapeDtypeStruct((2, outs, width), BF)] * 2
    else:
        out_shape = [jax.ShapeDtypeStruct((2, 6 * outs, width), F32)]
        aliases = {len(operands): 0}
    result = kernel_call(
        functools.partial(z_kernel, sources, last), scalars, operands, out_shape, aliases,
        (3, len(sources), LANES, width), 2 * 6 * outs * 6 * len(sources) * LANES * width,
    )
    return result if last else result[0]


def solution(mesh):
    bands, chans = mesh.shape["band"], mesh.shape["chan"]
    chips = chans // 2
    swap = [(2 * x + c, 2 * x + 1 - c) for x in range(chips) for c in range(2)]
    right = [(2 * x + c, 2 * ((x + 1) % chips) + c) for x in range(chips) for c in range(2)]
    left = [(target, source) for source, target in right]
    across = []
    for b in range(1, bands):
        for x in range(chips):
            here, there = b * chans + 2 * x + b % 2, (b - 1) * chans + 2 * x + b % 2
            across += [(here, there), (there, here)]
    across_last = list(across)
    for x in range(chips):
        here, there = 2 * x, (bands - 1) * chans + 2 * x + bands % 2
        across += [(here, there), (there, here)]
        across_last += [(here, 2 * (x ^ 1)), (there, there - 2 * x + 2 * (x ^ 1))]

    def on_device(new_frames, cached_frames, conv_weight, out_bias):
        index = lax.axis_index("chan")
        core, chip = index % 2, index // 2
        even = core == 0
        flip = (core + lax.axis_index("band")) % 2
        upper = flip == 0
        band = lax.axis_index("band")
        edge = jnp.where(upper, band == 0, band == bands - 1)

        def send(a, pairs, axes="chan"):
            return lax.ppermute(a, axes, pairs)

        def other_core(*pieces):
            return send(jnp.stack([piece[1] for piece in pieces]), swap)

        def next_band(pairs, *pieces):
            return send(jnp.stack([piece[0] for piece in pieces]), pairs, ("band", "chan"))

        scalars = jnp.stack([flip, edge.astype(flip.dtype)] + [(chip + o) % chips for o in (0, chips - 1, 1, 2)])
        scalars, upper, even = lax.optimization_barrier((scalars.astype(jnp.int32), upper, even))
        kept, sent = pack(scalars, cached_frames, new_frames)
        got = send(sent, swap)
        got, conv_weight, out_bias = lax.optimization_barrier((got, conv_weight, out_bias))
        other_weight = send(conv_weight, swap)
        biases = jnp.stack([out_bias, send(out_bias, swap)])
        biases, scalars = lax.optimization_barrier((biases, scalars))
        lo, hi = jnp.where(even, kept, got), jnp.where(even, got, kept)
        l_lo = send(lo, right)
        r_hi = send(hi, left)
        l_hi = send(hi, right)
        r_lo = send(lo, left)
        weights = (conv_weight, other_weight)

        z_own = next_band(across, lo, hi)
        acc = main_call(scalars, OWN, (lo, hi), other_core(lo, hi), weights, None, None)
        f_lo = send(l_lo, right)
        f_hi = send(r_hi, left)
        acc = main_call(scalars, LEFT_RIGHT, (l_lo, r_hi), other_core(l_lo, r_hi), weights, acc, None)
        z_sides = next_band(across, l_lo, r_hi, r_lo, l_hi)
        acc = main_call(scalars, RIGHT_LEFT, (r_lo, l_hi), other_core(r_lo, l_hi), weights, acc, None)
        z_far = next_band(across_last, f_lo, f_hi)
        acc, inner, inner_theirs = main_call(scalars, FAR, (f_lo, f_hi), other_core(f_lo, f_hi), weights, acc, biases)
        inner_given = send(inner_theirs, swap)
        sources = ((OWN, 0, 0), (LEFT_RIGHT, 1, 0), (RIGHT_LEFT, 1, 2))
        acc = z_call(scalars, sources, (z_own, z_sides), weights, acc, None)
        outer, outer_theirs = z_call(scalars, ((FAR, 0, 0),), (z_far,), weights, acc, biases)
        outer_given = send(outer_theirs, swap)
        return unpack(scalars, (outer, inner, outer_given, inner_given), new_frames.shape)

    in_specs = (
        P(None, "band", "chan", None),
        P(None, "band", "chan", None),
        P(None, None, None, "chan", None),
        P("chan"),
    )

    return jax.shard_map(
        on_device, mesh=mesh, in_specs=in_specs, out_specs=P(None, "band", "chan", None), check_vma=False
    )
```

```python
import functools

import jax
import jax.numpy as jnp
from jax import lax
from jax.experimental import pallas as pl
from jax.experimental.pallas import tpu as pltpu
from jax.sharding import PartitionSpec as P


BF = jnp.bfloat16
F32 = jnp.float32
LANES = 128
OWN, LEFT_RIGHT, RIGHT_LEFT, FAR = (2, 2), (3, 4), (4, 3), (5, 5)
HALF = 64


def turn(pairs):
    width = pairs.shape[-1]
    return pltpu.roll(pairs.astype(F32), width // 2, axis=1)


def pack_kernel(flip_ref, cached_ref, new_ref, kept_ref, sent_ref):
    cols = cached_ref.shape[-1]
    upper = flip_ref[0]
    place = [
        (lax.broadcasted_iota(jnp.int32, (cols, 2 * cols), 0) + h * cols
         == lax.broadcasted_iota(jnp.int32, (cols, 2 * cols), 1)).astype(F32).astype(BF)
        for h in range(2)
    ]
    for out, flip in ((kept_ref, upper), (sent_ref, 1 - upper)):
        for row in range(2):
            at = jnp.where(flip == 0, row, 3 - row)
            channels = cached_ref.shape[2]
            firsts = jnp.concatenate([cached_ref[0, at], new_ref[0, at], new_ref[2, at]], axis=0)
            seconds = jnp.concatenate([cached_ref[1, at], new_ref[1, at], new_ref[3, at]], axis=0)
            both = jnp.dot(firsts, place[0], preferred_element_type=F32)
            both = both + jnp.dot(seconds, place[1], preferred_element_type=F32)
            out[row] = both.astype(BF).reshape(3, channels, 2 * cols)


def pack(flip, cached, new):
    channels, cols = cached.shape[2:]
    shape = jax.ShapeDtypeStruct((2, 3, channels, 2 * cols), BF)
    return pl.pallas_call(
        pack_kernel,
        in_specs=[pl.BlockSpec(memory_space=pltpu.SMEM)] + [pl.BlockSpec(memory_space=pltpu.VMEM)] * 2,
        out_specs=[pl.BlockSpec(memory_space=pltpu.VMEM)] * 2,
        out_shape=[shape, shape],
        compiler_params=pltpu.CompilerParams(vmem_limit_bytes=16 * 2**20),
        cost_estimate=pl.CostEstimate(flops=10**8, bytes_accessed=4 * 2**20, transcendentals=0),
        name="pack",
    )(flip, cached, new)


def unpack_kernel(scalars, *refs):
    rows, (out, turned, sems) = refs[:4], refs[4:]
    cols = turned.shape[-1]
    copies = []
    for at, source in enumerate(rows):
        inner = at % 2
        lower = scalars[0] if at < 2 else 1 - scalars[0]
        row = jnp.where(lower == 0, inner, 3 - inner)
        for p in range(2):
            pair = source[p]
            turned[at, 2 * p] = pair[:, :cols]
            turned[at, 2 * p + 1] = turn(pair).astype(BF)[:, :cols]
            both = pl.ds(2 * p, 2)
            copies.append(pltpu.make_async_copy(turned.at[at, both], out.at[both, row], sems.at[at, p]))
            copies[-1].start()
    for copy in copies:
        copy.wait()


def unpack(scalars, rows, shape):
    vmem = pl.BlockSpec(memory_space=pltpu.VMEM)
    return pl.pallas_call(
        unpack_kernel,
        in_specs=[pl.BlockSpec(memory_space=pltpu.SMEM)] + [vmem] * 4,
        out_specs=pl.BlockSpec(memory_space=pltpu.HBM),
        out_shape=jax.ShapeDtypeStruct(shape, BF),
        scratch_shapes=[pltpu.VMEM((4, 4, *shape[2:]), BF), pltpu.SemaphoreType.DMA((4, 2))],
        compiler_params=pltpu.CompilerParams(vmem_limit_bytes=16 * 2**20),
        cost_estimate=pl.CostEstimate(flops=10**7, bytes_accessed=4 * 2**20, transcendentals=0),
        name="unpack",
    )(scalars, *rows)


def column_sum(acc, bias, cols):
    rows, width = acc.shape[0] // 6, acc.shape[1]
    lane = lax.broadcasted_iota(jnp.int32, (rows, width), 1)
    zero = jnp.zeros((rows, width), F32)
    left_edge = (lane == 0) | (lane == cols)
    right_edge = (lane == cols - 1) | (lane == width - 1)
    totals = []
    for half in range(2):
        part = acc[half * 3 * rows : (half + 1) * 3 * rows]
        from_left = jnp.where(left_edge, zero, pltpu.roll(part[:rows], 1, axis=1))
        from_right = jnp.where(right_edge, zero, pltpu.roll(part[2 * rows :], width - 1, axis=1))
        totals.append((part[rows : 2 * rows] + from_left + from_right + bias[half][:, None]).astype(BF))
    return totals


def tap_weights(scalars, blocks, weights, t, delta):
    lanes = [pl.ds(pl.multiple_of(scalars[at] * LANES, LANES), LANES) for at in blocks]
    row_tap = jnp.where(scalars[0] == 0, delta, 2 - delta)
    halves = []
    for half in range(2):
        w = weights[half][t, row_tap, :, :, lanes[0]]
        w = w.reshape(w.shape[0] * w.shape[1], LANES)
        if blocks[0] != blocks[1]:
            v = weights[half][t, row_tap, :, :, lanes[1]].reshape(w.shape)
            first = lax.broadcasted_iota(jnp.int32, (1, LANES), 1) < HALF
            w = jnp.where(jnp.broadcast_to(first, w.shape), w, v)
        halves.append(w)
    return jnp.concatenate(halves, axis=0)


def put_pairs(xs, at, low, high):
    near = lax.broadcasted_iota(jnp.int32, low.shape, 1) < low.shape[1] // 2
    xs[(0, *at)] = low
    xs[(2, *at)] = high
    xs[(1, *at)] = jnp.where(near, turn(low), turn(high)).astype(BF)


def main_kernel(blocks, first, last, *refs):
    scalars, lo, hi, csides, own, other, *refs = refs
    before = None if first else refs.pop(0)
    bias = refs.pop(0) if last else None
    buffers = refs.pop()
    cols = buffers.shape[-1] // 2

    def one_pair(p):
        xs = buffers.at[p]
        for piece, body in enumerate((lo, hi)):
            at = pl.ds(piece * HALF, HALF)
            for row in range(3):
                low, high = ((body[row, p], body[row, p + 1]) if row < 2 else (csides[piece, p], csides[piece, p + 1]))
                put_pairs(xs, (row, at), low, high)
        taps = {
            (t, delta): tap_weights(scalars, blocks, (own, other), t, delta) for t in range(3) for delta in range(3)
        }
        for row in range(2):
            used = [at for at in taps if row + at[1] >= 1]
            lhs = jnp.concatenate([taps[at] for at in used], axis=1)
            window = jnp.concatenate([xs[t, row + delta - 1] for t, delta in used], axis=0)
            acc = jnp.dot(lhs, window, preferred_element_type=F32)
            if not first:
                acc = acc + before[p, row]
            if not last:
                refs[0][p, row] = acc
            elif row == 0:
                refs[0][p] = acc
            else:
                refs[1][p], refs[2][p] = column_sum(acc, bias, cols)

    for p in range(2):
        one_pair(p)


def z_kernel(sources, last, *refs):
    scalars, *refs = refs
    zs = [refs.pop(0) for _ in range(1 + max(which for _, which, _ in sources))]
    own, other, before = refs[:3]
    refs = refs[3:]
    bias = refs.pop(0) if last else None
    buffers = refs.pop()
    width = buffers.shape[-1]
    edge = scalars[1] == 1

    def one_pair(p):
        xs = buffers.at[p]
        lhs, window = [], []
        for slot, (blocks, which, start) in enumerate(sources):
            for piece in range(2):
                low, high = (
                    jnp.where(edge, jnp.zeros((HALF, width), BF), zs[which][start + piece, q]) for q in (p, p + 1)
                )
                put_pairs(xs, (slot, pl.ds(piece * HALF, HALF)), low, high)
            for t in range(3):
                lhs.append(tap_weights(scalars, blocks, (own, other), t, 0))
                window.append(xs[t, slot])
        acc = before[p] + jnp.dot(
            jnp.concatenate(lhs, axis=1), jnp.concatenate(window, axis=0), preferred_element_type=F32
        )
        if last:
            refs[0][p], refs[1][p] = column_sum(acc, bias, width // 2)
        else:
            refs[0][p] = acc

    for p in range(2):
        one_pair(p)


def kernel_call(body, scalars, operands, out_shape, aliases, scratch, flops):
    vmem = pl.BlockSpec(memory_space=pltpu.VMEM)
    return pl.pallas_call(
        body,
        in_specs=[pl.BlockSpec(memory_space=pltpu.SMEM)] + [vmem] * len(operands),
        out_specs=[vmem] * len(out_shape),
        scratch_shapes=[pltpu.VMEM(scratch, BF)],
        out_shape=out_shape,
        input_output_aliases=aliases,
        compiler_params=pltpu.CompilerParams(vmem_limit_bytes=28 * 2**20),
        cost_estimate=pl.CostEstimate(flops=flops, bytes_accessed=8 * 2**20, transcendentals=0),
    )(scalars, *operands)


def main_call(scalars, blocks, bodies, csides, weights, before, bias):
    first, last = before is None, bias is not None
    outs, width = weights[0].shape[3], csides.shape[-1]
    operands = [*bodies, csides, *weights]
    aliases = {}
    if last:
        operands += [before, bias]
        out_shape = [jax.ShapeDtypeStruct((2, 6 * outs, width), F32)] + [jax.ShapeDtypeStruct((2, outs, width), BF)] * 2
    else:
        out_shape = [jax.ShapeDtypeStruct((2, 2, 6 * outs, width), F32)]
        if not first:
            operands.append(before)
            aliases = {len(operands): 0}
    result = kernel_call(
        functools.partial(main_kernel, blocks, first, last), scalars, operands, out_shape, aliases,
        (2, 3, 3, LANES, width), 2 * 6 * outs * 30 * LANES * width,
    )
    return result if last else result[0]


def z_call(scalars, sources, zs, weights, before, bias):
    last = bias is not None
    outs, width = weights[0].shape[3], before.shape[-1]
    operands = [*zs, *weights, before]
    aliases = {}
    if last:
        operands.append(bias)
        out_shape = [jax.ShapeDtypeStruct((2, outs, width), BF)] * 2
    else:
        out_shape = [jax.ShapeDtypeStruct((2, 6 * outs, width), F32)]
        aliases = {len(operands): 0}
    result = kernel_call(
        functools.partial(z_kernel, sources, last), scalars, operands, out_shape, aliases,
        (2, 3, len(sources), LANES, width), 2 * 6 * outs * 6 * len(sources) * LANES * width,
    )
    return result if last else result[0]


def solution(mesh):
    bands, chans = mesh.shape["band"], mesh.shape["chan"]
    chips = chans // 2
    swap = [(2 * x + c, 2 * x + 1 - c) for x in range(chips) for c in range(2)]
    right = [(2 * x + c, 2 * ((x + 1) % chips) + c) for x in range(chips) for c in range(2)]
    left = [(target, source) for source, target in right]
    across = []
    for b in range(1, bands):
        for x in range(chips):
            here, there = b * chans + 2 * x + b % 2, (b - 1) * chans + 2 * x + b % 2
            across += [(here, there), (there, here)]
    across_last = list(across)
    for x in range(chips):
        here, there = 2 * x, (bands - 1) * chans + 2 * x + bands % 2
        across += [(here, there), (there, here)]
        across_last += [(here, 2 * (x ^ 1)), (there, there - 2 * x + 2 * (x ^ 1))]

    def on_device(new_frames, cached_frames, conv_weight, out_bias):
        index = lax.axis_index("chan")
        core, chip = index % 2, index // 2
        even = core == 0
        flip = (core + lax.axis_index("band")) % 2
        upper = flip == 0
        band = lax.axis_index("band")
        edge = jnp.where(upper, band == 0, band == bands - 1)

        def send(a, pairs, axes="chan"):
            return lax.ppermute(a, axes, pairs)

        def other_core(*pieces):
            return send(jnp.stack([piece[1] for piece in pieces]), swap)

        def next_band(pairs, *pieces):
            return send(jnp.stack([piece[0] for piece in pieces]), pairs, ("band", "chan"))

        scalars = jnp.stack([flip, edge.astype(flip.dtype)] + [(chip + o) % chips for o in (0, chips - 1, 1, 2)])
        scalars, upper, even = lax.optimization_barrier((scalars.astype(jnp.int32), upper, even))
        kept, sent = pack(scalars, cached_frames, new_frames)
        got = send(sent, swap)
        got, conv_weight, out_bias = lax.optimization_barrier((got, conv_weight, out_bias))
        other_weight = send(conv_weight, swap)
        biases = jnp.stack([out_bias, send(out_bias, swap)])
        biases, scalars = lax.optimization_barrier((biases, scalars))
        lo, hi = jnp.where(even, kept, got), jnp.where(even, got, kept)
        l_lo = send(lo, right)
        r_hi = send(hi, left)
        l_hi = send(hi, right)
        r_lo = send(lo, left)
        weights = (conv_weight, other_weight)

        z_own = next_band(across, lo, hi)
        acc = main_call(scalars, OWN, (lo, hi), other_core(lo, hi), weights, None, None)
        f_lo = send(l_lo, right)
        f_hi = send(r_hi, left)
        acc = main_call(scalars, LEFT_RIGHT, (l_lo, r_hi), other_core(l_lo, r_hi), weights, acc, None)
        z_sides = next_band(across, l_lo, r_hi, r_lo, l_hi)
        acc = main_call(scalars, RIGHT_LEFT, (r_lo, l_hi), other_core(r_lo, l_hi), weights, acc, None)
        z_far = next_band(across_last, f_lo, f_hi)
        acc, inner, inner_theirs = main_call(scalars, FAR, (f_lo, f_hi), other_core(f_lo, f_hi), weights, acc, biases)
        inner_given = send(inner_theirs, swap)
        sources = ((OWN, 0, 0), (LEFT_RIGHT, 1, 0), (RIGHT_LEFT, 1, 2))
        acc = z_call(scalars, sources, (z_own, z_sides), weights, acc, None)
        outer, outer_theirs = z_call(scalars, ((FAR, 0, 0),), (z_far,), weights, acc, biases)
        outer_given = send(outer_theirs, swap)
        return unpack(scalars, (outer, inner, outer_given, inner_given), new_frames.shape)

    in_specs = (
        P(None, "band", "chan", None),
        P(None, "band", "chan", None),
        P(None, None, None, "chan", None),
        P("chan"),
    )

    return jax.shard_map(
        on_device, mesh=mesh, in_specs=in_specs, out_specs=P(None, "band", "chan", None), check_vma=False
    )
```
